32 devices in a mesh: dom: 8 (over z, x), band: 4 (over y, core).
Axes of the slice: x: 2, y: 2, z: 4, core: 2. Of those that a mesh axis runs over, the one named last changes fastest.
Arguments:
- orbitals: float32 [1280, 16, 8, 128], P('band', 'dom'), may hold values from -12 to 12, as said below
- potential: float32 [16, 8, 128], P('dom'), may hold values from -2 to 0
Outputs:
- filtered: float32 [1280, 16, 8, 128], P('band', 'dom')
The draws below stay inside these ranges and needn't reach their ends.
Inputs may be any that keep to these rules, and one draw needn't show every extreme that they name: real-valued orbitals.
All inputs are finite; a program needn't handle non-finite values.
Results may differ from the reference program's by a relative error of at most 0.00029.
Values sent between devices are 32-bit elements; how exact they have to be, the bound alone decides.
No kernel may reach another device: no remote copies, remote signals or barrier semaphores. Data moves between devices by JAX's collectives and lax.ppermute only.
A program may use at most 192 MiB of HBM per device.

```python
import jax
import jax.numpy as jnp
from jax import lax

ORB_DEV = 320
PANEL = 64
PANELS = 3
NS_ITERS = 16
CY = 8
CZ = 128
NORB = 1280
NX = 16
N_BAND = 4


def draw_orbitals(key, part):
    key_base = jax.random.fold_in(key, 11)
    key_common = jax.random.fold_in(key, 12)
    key_weight = jax.random.fold_in(key, 13)
    common = jnp.clip(jax.random.normal(key_common, (NX, CY, CZ), jnp.float32), -5.0, 5.0)
    weights = jax.random.uniform(key_weight, (NORB, 1, 1, 1), jnp.float32, 0.3, 1.0)
    base = jnp.clip(jax.random.normal(key_base, (NORB, NX, CY, CZ), jnp.float32), -5.0, 5.0)
    return base + weights * common


def shard_levels(own_key, dims, cuts, low, high):
    def one(dim, blocks):
        steps = jax.random.uniform(jax.random.fold_in(jax.random.fold_in(own_key, 6), dim), (blocks,), jnp.float32, low / len(cuts), high / len(cuts))
        return jnp.repeat(jnp.exp(steps), dims[dim] // blocks).reshape((-1,) + (1,) * (len(dims) - dim - 1))

    loudness = one(*cuts[0])
    for cut in cuts[1:]:
        loudness = loudness * one(*cut)
    return loudness


def setup_inputs(seed: int = 0) -> dict:
    splits = jax.random.split(jax.random.key(seed), 3)
    orbitals = draw_orbitals(jax.random.fold_in(splits[2], 71), 0)
    potential = jnp.clip(-2.0 + 2.0 * jax.random.uniform(splits[1], (NX, CY, CZ), jnp.float32) ** shard_levels(splits[1], (NX, CY, CZ), ((0, 8),), -0.2, 0.2), -2.0, 0.0)
    return {"orbitals": orbitals, "potential": potential}


SHIFT = 1.0
HALF = 1.5

def hdot(left, right):
    return jnp.dot(left, right, precision=lax.Precision.HIGHEST, preferred_element_type=jnp.float32)

def rolled(values, offset, which):
    return jnp.roll(values, offset, axis=which)

def apply_h(field_pad, potential_pad):
    centre = field_pad[:, 1:-1]
    upper = field_pad[:, 2:]
    lower = field_pad[:, :-2]
    face_sum = upper + lower + rolled(centre, 1, 2) + rolled(centre, -1, 2) + rolled(centre, 1, 3) + rolled(centre, -1, 3)
    edge_sum = jnp.zeros_like(centre)
    for offset in (1, -1):
        edge_sum = edge_sum + rolled(upper, offset, 2) + rolled(lower, offset, 2) + rolled(upper, offset, 3) + rolled(lower, offset, 3)
        for second in (1, -1):
            edge_sum = edge_sum + rolled(rolled(centre, offset, 2), second, 3)
    laplace = (2.0 * face_sum + edge_sum - 24.0 * centre) / 6.0
    weighted = potential_pad[None] * field_pad
    middle = weighted[:, 1:-1]
    near_sum = weighted[:, 2:] + weighted[:, :-2] + rolled(middle, 1, 2) + rolled(middle, -1, 2) + rolled(middle, 1, 3) + rolled(middle, -1, 3)
    return -0.5 * laplace + 0.5 * middle + near_sum / 12.0

def inv_sqrt(correlation):
    order = correlation.shape[0]
    eye = jnp.eye(order, dtype=jnp.float32)
    scale = jnp.sqrt(jnp.sum(correlation * correlation))
    root = correlation / scale
    inverse = eye
    for turn in range(NS_ITERS):
        factor = 0.5 * (3.0 * eye - hdot(inverse, root))
        root = hdot(root, factor)
        inverse = hdot(factor, inverse)
    return inverse / jnp.sqrt(scale)

def reference(orbitals, potential):
    potential_pad = jnp.concatenate([potential[-1:], potential, potential[:1]], axis=0)

    def filter_block(block):
        padded = jnp.concatenate([block[:, -1:], block, block[:, :1]], axis=1)
        first = (apply_h(padded, potential_pad) - SHIFT * block) / HALF
        padded_first = jnp.concatenate([first[:, -1:], first, first[:, :1]], axis=1)
        return 2.0 * (apply_h(padded_first, potential_pad) - SHIFT * first) / HALF - block
    grouped = orbitals.reshape(N_BAND, ORB_DEV, NX, CY, CZ)
    swept = lax.map(filter_block, grouped)
    blocks = [swept[index].reshape(ORB_DEV, NX * CY * CZ) for index in range(N_BAND)]
    local_row = jnp.arange(ORB_DEV)
    for panel_index in range(PANELS):
        panel = blocks[panel_index][:PANEL]
        weights = inv_sqrt(hdot(panel, panel.T))
        basis = hdot(weights, panel)
        for index in range(N_BAND):
            coeffs = hdot(basis, blocks[index].T)
            if index <= panel_index:
                keep = jnp.where(local_row < PANEL, 0.0, 1.0).astype(jnp.float32)
            else:
                keep = jnp.ones((ORB_DEV,), jnp.float32)
            updated = blocks[index] - keep[:, None] * hdot(coeffs.T, basis)
            if index == panel_index:
                updated = updated.at[:PANEL].set(basis)
            blocks[index] = updated
    return jnp.stack(blocks).reshape(NORB, NX, CY, CZ)
```

```python
import jax
import jax.numpy as jnp
from jax import lax
from jax.experimental import pallas as pl
from jax.experimental.pallas import tpu as pltpu
from jax.sharding import PartitionSpec as P

PANEL = 64
PANELS = 3
NS_ITERS = 16
SHIFT = 1.0
HALF = 1.5
CHUNKS = 2
ROWS = 16


f32 = jnp.float32
bf16 = jnp.bfloat16


def ring_sum(tile, axis):
    size = tile.shape[axis]
    return pltpu.roll(tile, 1, axis) + pltpu.roll(tile, size - 1, axis)


def shifted_h(tiles, fields, scale, base=None):
    products = [field[0] * tile for field, tile in zip(fields, tiles)]
    out = []
    for i in range(1, len(tiles) - 1):
        tile = tiles[i]
        pair = tiles[i - 1] + tiles[i + 1]
        lane = ring_sum(tile, 1)
        rest = fields[i][1] * tile - pair
        total = fields[i][2] * tile + (products[i - 1] + products[i + 1]) - (pair + pair)
        total = total + ring_sum(rest, 1) + ring_sum(rest - lane, 0)
        total = total * (scale / 12.0)
        out.append(total if base is None else total - base[i])
    return out


def layer_fields(pot_ref, parity, slots, depth):
    fields = []
    for slot in range(slots):
        for j in range(depth):
            v = pot_ref[slot, jnp.where(parity == 0, j, depth - 1 - j)]
            fields.append((v, v - 2.0, v * 6.0 + (24.0 - 12.0 * SHIFT)))
    return fields


def filter_rows(row, sources, fields, parity, depth):
    tiles = []
    for ref in sources:
        for j in range(depth):
            tiles.append(ref[row, jnp.where(parity == 0, j, depth - 1 - j)])
    first = shifted_h(tiles, fields, 1.0 / HALF)
    second = shifted_h(first, fields[1:-1], 2.0 / HALF, base=tiles[1:-1])
    return second


def filter_kernel(slots, depth, kept, info_ref, *refs):
    sources, pot_ref, outs = refs[:slots], refs[slots], refs[slots + 1 :]
    parity = info_ref[0]
    fields = layer_fields(pot_ref, parity, slots, depth)
    count = sources[0].shape[0]

    def step(row, carry):
        second = filter_rows(row, sources, fields, parity, depth)
        for out, slot in zip(outs, kept):
            for j in range(depth):
                out[row, jnp.where(parity == 0, j, depth - 1 - j)] = second[slot * depth + j - 2]
        return carry

    lax.fori_loop(0, count, step, 0, unroll=2)


def run_filter(info, sources, starts, pots, kept, rows):
    depth, cy, cz = sources[0].shape[1:]
    slots = len(sources)
    block = (ROWS, depth, cy, cz)

    def source_spec(start):
        return pl.BlockSpec(block, lambda i, info_ref: (start(info_ref) + i, 0, 0, 0))

    in_specs = [source_spec(s) for s in starts]
    in_specs.append(pl.BlockSpec((slots, depth, cy, cz), lambda i, info_ref: (0, 0, 0, 0)))
    out_spec = pl.BlockSpec(block, lambda i, info_ref: (i, 0, 0, 0))
    tiles = rows * depth
    return pl.pallas_call(
        lambda *refs: filter_kernel(slots, depth, kept, *refs),
        out_shape=[jax.ShapeDtypeStruct((rows, depth, cy, cz), f32)] * len(kept),
        grid_spec=pltpu.PrefetchScalarGridSpec(
            num_scalar_prefetch=1,
            grid=(rows // ROWS,),
            in_specs=in_specs,
            out_specs=[out_spec] * len(kept),
        ),
        cost_estimate=pl.CostEstimate(
            flops=tiles * 1024 * 100, bytes_accessed=tiles * 4096 * (slots + len(kept)), transcendentals=0
        ),
        name="filter%d" % slots,
    )(info, *sources, pots)


def split2(a):
    h = a.astype(bf16)
    m = (a - h.astype(f32)).astype(bf16)
    return h, m


def split3(a):
    h = a.astype(bf16)
    r = a - h.astype(f32)
    m = r.astype(bf16)
    low = (r - m.astype(f32)).astype(bf16)
    return h, m, low


def mm(a, b, dims=((1,), (0,))):
    return lax.dot_general(a, b, (dims, ((), ())), preferred_element_type=f32)


def exact(a, b):
    ah, am, al = split3(a)
    bh, bm, bl = split3(b)
    small = mm(jnp.concatenate([ah, am, am, ah], 1), jnp.concatenate([bm, bh, bm, bl], 0))
    return mm(ah, bh) + small + mm(al, bh)


def hdot(a, b):
    return jnp.dot(a, b, precision=lax.Precision.HIGHEST, preferred_element_type=f32)


def gram_kernel(count, cells, info_ref, *refs):
    slots, (mat_ref, gram_ref) = refs[:count], refs[count:]
    band = info_ref[1]
    for k in range(PANELS):
        for j in range(count):

            @pl.when(band ^ k == j)
            def _():
                for c in range(cells):
                    mat_ref[k * PANEL : (k + 1) * PANEL, c * 128 : (c + 1) * 128] = slots[j][
                        pl.ds(c, PANEL, stride=cells), :
                    ]

    h, m = split2(mat_ref[...])
    left = jnp.concatenate([h, h, m], 1)
    right = jnp.concatenate([h, m, h], 1)
    gram_ref[...] = mm(left, right, ((1,), (1,)))


def run_gram(info, slots, cells):
    width = PANEL * PANELS
    vmem = pl.BlockSpec(memory_space=pltpu.VMEM)
    return pl.pallas_call(
        lambda *refs: gram_kernel(len(slots), cells, *refs),
        out_shape=[jax.ShapeDtypeStruct((width, cells * 128), f32), jax.ShapeDtypeStruct((width, width), f32)],
        in_specs=[pl.BlockSpec(memory_space=pltpu.SMEM)] + [vmem] * len(slots),
        out_specs=[vmem, vmem],
        cost_estimate=pl.CostEstimate(
            flops=6 * width * width * cells * 128, bytes_accessed=width * cells * 128 * 8, transcendentals=0
        ),
        name="gram",
    )(info, *[s.reshape(-1, 128) for s in slots])


def tracked_kernel(count, rows, cells, info_ref, mat_ref, *refs):
    sources, (out_ref, scratch) = refs[:count], refs[count:]
    h, m = split2(mat_ref[...])
    right = jnp.concatenate([h, m, h], 1)
    for i in range(count):
        for c in range(cells):
            scratch[:, c * 128 : (c + 1) * 128] = sources[i][pl.ds(c, rows, stride=cells), :]
        lh, lm = split2(scratch[...])
        place = jnp.where(info_ref[0] == 0, i, count - 1 - i)
        out_ref[pl.ds(pl.multiple_of(place * rows, rows), rows), :] = mm(
            jnp.concatenate([lh, lh, lm], 1), right, ((1,), (1,))
        )


def run_tracked(info, mat, sources, cells):
    width = mat.shape[0]
    rows = sources[0].shape[0]
    vmem = pl.BlockSpec(memory_space=pltpu.VMEM)
    return pl.pallas_call(
        lambda *refs: tracked_kernel(len(sources), rows, cells, *refs),
        out_shape=jax.ShapeDtypeStruct((rows * len(sources), width), f32),
        in_specs=[pl.BlockSpec(memory_space=pltpu.SMEM)] + [vmem] * (1 + len(sources)),
        out_specs=vmem,
        scratch_shapes=[pltpu.VMEM((rows, cells * 128), f32)],
        cost_estimate=pl.CostEstimate(
            flops=6 * width * rows * len(sources) * cells * 128,
            bytes_accessed=(width + rows) * cells * 128 * 4,
            transcendentals=0,
        ),
        name="tracked",
    )(info, mat, *[s.reshape(-1, 128) for s in sources])


def eye(n):
    i0 = lax.broadcasted_iota(jnp.int32, (n, n), 0)
    i1 = lax.broadcasted_iota(jnp.int32, (n, n), 1)
    return jnp.where(i0 == i1, 1.0, 0.0).astype(f32)


def inv_sqrt(correlation):
    one = eye(correlation.shape[0])
    scale = jnp.sqrt(jnp.sum(correlation * correlation, keepdims=True))

    def turn(_, carry):
        root, inverse = carry
        factor = 0.5 * (3.0 * one - exact(inverse, root))
        return exact(root, factor), exact(factor, inverse)

    _, inverse = lax.fori_loop(0, NS_ITERS, turn, (correlation / scale, one))
    return inverse / jnp.sqrt(scale)


def chain_kernel(info_ref, gram_ref, mat_ref, theta_ref, basis_ref, factor_ref):
    band = info_ref[1]
    gram = gram_ref[...]
    width = gram.shape[0]
    one = eye(width)
    factors, images = [], []
    remain = one
    mix = jnp.zeros((width, width), f32)
    for k in range(PANELS):
        current = one[k * PANEL : (k + 1) * PANEL]
        for factor, image in zip(factors, images):
            current = current - exact(exact(current, image.T), factor)
        correlation = exact(exact(current, gram), current.T)
        factor = exact(inv_sqrt(correlation), current)
        image = exact(factor, gram)
        coeffs = exact(factor, remain)
        remain = remain - exact(image.T, coeffs)
        mix = mix + exact(coeffs.T, factor)
        factors.append(factor)
        images.append(image)
        factor_ref[k * PANEL : (k + 1) * PANEL, :] = factor
    h, m = split2(mat_ref[...])
    right = jnp.concatenate([h, m, h], 0)
    mh, mlow = split2(mix)
    theta_ref[...] = mm(jnp.concatenate([mh, mh, mlow], 1), right)
    own = jnp.minimum(band, PANELS - 1) * PANEL
    oh, om = split2(factor_ref[pl.ds(pl.multiple_of(own, PANEL), PANEL), :])
    basis_ref[...] = mm(jnp.concatenate([oh, oh, om], 1), right)


def run_chain(info, gram, mat):
    width, cells = mat.shape
    vmem = pl.BlockSpec(memory_space=pltpu.VMEM)
    return pl.pallas_call(
        chain_kernel,
        out_shape=[jax.ShapeDtypeStruct((width, cells), f32), jax.ShapeDtypeStruct((PANEL, cells), f32)],
        in_specs=[pl.BlockSpec(memory_space=pltpu.SMEM), vmem, vmem],
        out_specs=[vmem, vmem],
        scratch_shapes=[pltpu.VMEM((width, width), f32)],
        cost_estimate=pl.CostEstimate(flops=10**9, bytes_accessed=10**7, transcendentals=0),
        name="chain",
    )(info, gram, mat)


def piece_row(i, info_ref):
    half = (i - 1) % 2
    swapped = jnp.where(info_ref[0] == 0, half, 1 - half)
    return jnp.where(i == 0, 0, i - half + swapped)


def update_kernel(pieces, cells, info_ref, basis_ref, theta_ref, tracked_ref, *refs):
    sources, out_ref = refs[:pieces], refs[pieces]
    step = pl.program_id(0)
    for i in range(pieces):

        @pl.when(step == i)
        def _():
            rows = sources[i].shape[0] // cells
            th, tm = split2(theta_ref[...])
            place = piece_row(i, info_ref) * rows
            lh, lm = split2(tracked_ref[pl.ds(pl.multiple_of(place, rows), rows), :])
            change = mm(jnp.concatenate([lh, lh, lm], 1), jnp.concatenate([th, tm, th], 0))
            for c in range(cells):
                value = sources[i][pl.ds(c, rows, stride=cells), :] - change[:, c * 128 : (c + 1) * 128]
                if i == 0:
                    value = jnp.where(info_ref[1] < PANELS, basis_ref[:, c * 128 : (c + 1) * 128], value)
                out_ref[pl.ds(c, rows, stride=cells), :] = value


def run_update(info, basis, theta, tracked, sources, shape, cells):
    pieces = len(sources)
    rows = sources[0].shape[0]

    def whole(array):
        return pl.BlockSpec(array.shape, lambda i, info_ref: (0,) * array.ndim)

    def out_map(i, info_ref):
        return (piece_row(i, info_ref), 0)

    flat = [s.reshape(-1, 128) for s in sources]
    out = pl.pallas_call(
        lambda *refs: update_kernel(pieces, cells, *refs),
        out_shape=jax.ShapeDtypeStruct((shape[0] * cells, 128), f32),
        grid_spec=pltpu.PrefetchScalarGridSpec(
            num_scalar_prefetch=1,
            grid=(pieces,),
            in_specs=[whole(basis), whole(theta), whole(tracked)] + [whole(s) for s in flat],
            out_specs=pl.BlockSpec((rows * cells, 128), out_map),
        ),
        cost_estimate=pl.CostEstimate(
            flops=6 * shape[0] * theta.shape[0] * cells * 128,
            bytes_accessed=2 * shape[0] * cells * 512,
            transcendentals=0,
        ),
        name="update",
    )(info, basis, theta, tracked, *flat)
    return out.reshape(shape)


def per_device(orbitals, potential):
    count, depth, cy, cz = orbitals.shape
    cells = depth * cy
    doms = lax.axis_size("dom")
    bands = lax.axis_size("band")
    dom = lax.axis_index("dom")
    band = lax.axis_index("band")
    parity = dom % 2
    info = jnp.stack([parity, band]).astype(jnp.int32)

    mate = [(i, i ^ 1) for i in range(doms)]
    other = [(i, (i + 1 if i % 2 else i - 1) % doms) for i in range(doms)]
    outward = [(i, (i + 2 if i % 2 else i - 2) % doms) for i in range(doms)]
    inward = [(i, (i - 2 if i % 2 else i + 2) % doms) for i in range(doms)]

    def send(value, pairs, axis="dom"):
        return lax.ppermute(value, axis, pairs)

    head = jnp.concatenate([orbitals[:PANEL], potential[None]], axis=0)
    head_mate = send(head, mate)
    head_other = send(head, other)

    width = (count - PANEL) // CHUNKS
    half = width // 2
    mated, outer, inner = [], [], []
    for c in range(CHUNKS):
        base = PANEL + c * width
        mated.append(send(lax.dynamic_slice_in_dim(orbitals, base + (1 - parity) * half, half), mate))
    for c in range(CHUNKS):
        base = PANEL + c * width
        mine = lax.dynamic_slice_in_dim(orbitals, base + parity * half, half)
        if c == 0:
            mine = jnp.concatenate([mine, potential[None]], axis=0)
        outer.append(send(mine, outward))
        inner.append(send(mated[c], inward))

    near = jnp.stack([head_other[PANEL], potential, head_mate[PANEL]])
    (panel,) = run_filter(
        info, [head_other, orbitals, head_mate], [lambda r: 0] * 3, near, [1], PANEL
    )
    pots = jnp.concatenate([near, outer[0][half:]], axis=0)

    slots = [panel]
    bit = bands // 2
    order = [0]
    while bit:
        pairs = [(i, i ^ bit) for i in range(bands)]
        slots = slots + [send(s, pairs, "band") for s in slots]
        order = order + [o ^ bit for o in order]
        bit //= 2
    by_slot = [None] * bands
    for o, s in zip(order, slots):
        by_slot[o] = s
    mat, gram = run_gram(info, by_slot, cells)

    def total(value):
        step = 1
        while step < doms:
            value = value + send(value, [(i, i ^ step) for i in range(doms)])
            step *= 2
        return value

    gram = total(gram)

    pieces = [panel]
    tracked = [total(run_tracked(info, mat, [panel], cells))]
    for c in range(CHUNKS):
        start = (PANEL + c * width) // ROWS
        step = half // ROWS

        def mine_start(r, start=start, step=step):
            return start + r[0] * step

        own, theirs = run_filter(
            info,
            [inner[c], orbitals, mated[c], outer[c]],
            [lambda r: 0, mine_start, lambda r: 0, lambda r: 0],
            pots,
            [1, 2],
            half,
        )
        back = send(theirs, mate)
        pieces += [own, back]
        tracked.append(total(run_tracked(info, mat, [own, back], cells)))
    theta, basis = run_chain(info, gram, mat)
    return run_update(info, basis, theta, jnp.concatenate(tracked, axis=0), pieces, orbitals.shape, cells)


def solution(mesh):
    in_specs = (P("band", "dom", None, None), P("dom", None, None))
    out_specs = P("band", "dom", None, None)
    return jax.shard_map(
        per_device, mesh=mesh, in_specs=in_specs, out_specs=out_specs, check_vma=False
    )
```
